32 devices in a mesh: seq: 8 (over y, x, core), fsdp: 4 (over z).
Axes of the slice: x: 2, y: 2, z: 4, core: 2. Of those that a mesh axis runs over, the one named last changes fastest.
Arguments:
- inputs: bfloat16 [16, 3136, 512], P('fsdp', 'seq'), may hold values from -6 to 6
- cotangent: bfloat16 [16, 3136, 512], P('fsdp', 'seq'), may hold values from -6 to 6
- region_ids: int32 [56, 56], replicated, may hold values from 0 to 2
- rel_index: int32 [49, 49], replicated, may hold values from 0 to 168
- ln1_gain: float32 [2, 512], replicated, may hold values from 0.5 to 1.5
- ln1_bias: float32 [2, 512], replicated, may hold values from -3 to 3
- qkv_w: bfloat16 [2, 512, 1536], P(None, 'fsdp'), may hold values from -0.25 to 0.25
- q_bias: float32 [2, 512], replicated, may hold values from -3 to 3
- v_bias: float32 [2, 512], replicated, may hold values from -3 to 3
- rel_table: float32 [2, 169, 16], replicated, may hold values from -4 to 4
- proj_w: bfloat16 [2, 512, 512], P(None, 'fsdp'), may hold values from -1.5 to 1.5
- proj_b: float32 [2, 512], replicated, may hold values from -3 to 3
- ln2_gain: float32 [2, 512], replicated, may hold values from 0.5 to 1.5
- ln2_bias: float32 [2, 512], replicated, may hold values from -3 to 3
- fc1_w: bfloat16 [2, 512, 2048], P(None, 'fsdp'), may hold values from -0.25 to 0.25
- fc1_b: float32 [2, 2048], replicated, may hold values from -3 to 3
- fc2_w: bfloat16 [2, 2048, 512], P(None, 'fsdp'), may hold values from -0.125 to 0.125
- fc2_b: float32 [2, 512], replicated, may hold values from -3 to 3
Outputs:
- out: float32 [16, 3136, 512], P('fsdp', 'seq')
- grad_inputs: float32 [16, 3136, 512], P('fsdp', 'seq')
- grad_ln1_gain: float32 [2, 512], replicated
- grad_ln1_bias: float32 [2, 512], replicated
- grad_qkv_w: float32 [2, 512, 1536], P(None, 'fsdp')
- grad_q_bias: float32 [2, 512], replicated
- grad_v_bias: float32 [2, 512], replicated
- grad_rel_table: float32 [2, 169, 16], replicated
- grad_proj_w: float32 [2, 512, 512], P(None, 'fsdp')
- grad_proj_b: float32 [2, 512], replicated
- grad_ln2_gain: float32 [2, 512], replicated
- grad_ln2_bias: float32 [2, 512], replicated
- grad_fc1_w: float32 [2, 512, 2048], P(None, 'fsdp')
- grad_fc1_b: float32 [2, 2048], replicated
- grad_fc2_w: float32 [2, 2048, 512], P(None, 'fsdp')
- grad_fc2_b: float32 [2, 512], replicated
The draws below stay inside these ranges and needn't reach their ends.
Inputs may be any that keep to these rules, and one draw needn't show every extreme that they name: `region_ids`: region labels; in a shifted block a token attends only to tokens of its window with the same label. `rel_index`: each entry names a row of the relative-bias tables.
All inputs are finite; a program needn't handle non-finite values.
Results may differ from the reference program's by a relative error of at most 0.019.
Values may be sent and summed in bfloat16 or wider, within the bound.
No kernel may reach another device: no remote copies, remote signals or barrier semaphores. Data moves between devices by JAX's collectives and lax.ppermute only.
A program may use at most 320 MiB of HBM per device.

```python
import jax
import jax.numpy as jnp
from jax import lax

C = 512
HEADS = 16
FF = 2048
WIN = 7
SHIFT = 3
WIN2 = 49
BIAS_ROWS = 169
SIDE = 56
HW = 3136
LAYERS = 2
IMAGES = 16


def place_ends(values, rng, least, high):
    longest = values.shape.index(max(values.shape))
    spots = []
    for shift in (0, 1):
        where = [jax.random.randint(jax.random.fold_in(rng, axis), (), 0, length) for axis, length in enumerate(values.shape)]
        where[longest] = (where[longest] + shift) % values.shape[longest]
        spots.append(tuple(where))
    return values.at[spots[0]].set(least).at[spots[1]].set(high)


def level_of(stream_key, dims, split, least, top_value):
    factor_of = 1.0
    for axis_at, shards_of in split:
        heights = jax.random.uniform(jax.random.fold_in(jax.random.fold_in(stream_key, 6), axis_at), (shards_of,), jnp.float32, least / len(split), top_value / len(split))
        factor_of = factor_of * jnp.repeat(jnp.exp(heights), dims[axis_at] // shards_of).reshape((-1,) + (1,) * (len(dims) - 1 - axis_at))
    return factor_of


def centred(stream_key, extent, deviation, most, cuts=(), dtype=jnp.bfloat16):
    drawn = jax.random.normal(stream_key, extent, jnp.float32) * deviation
    if len(cuts) > 0:
        drawn = level_of(stream_key, extent, cuts, -0.22, 0.18) * drawn
    return jnp.clip(drawn, min=-most, max=most).astype(dtype)


def setup_inputs(seed: int = 0) -> dict:
    key_list = jax.random.split(jax.random.key(seed), 19)
    return {
        "inputs": centred(key_list[0], (IMAGES, HW, C), 1.0, 6.0, ((0, 4), (1, 8))),
        "cotangent": centred(key_list[1], (IMAGES, HW, C), 1.0, 6.0, ((0, 4), (1, 8))),
        "region_ids": place_ends(jax.random.randint(key_list[2], (SIDE, SIDE), 0, 3), jax.random.fold_in(key_list[2], 1), 0, 2).astype(jnp.int32),
        "rel_index": place_ends(jax.random.randint(key_list[3], (WIN2, WIN2), 0, BIAS_ROWS), jax.random.fold_in(key_list[3], 1), 0, BIAS_ROWS - 1).astype(jnp.int32),
        "ln1_gain": jnp.clip(1.0 + 0.1 * jax.random.normal(key_list[4], (LAYERS, C), jnp.float32), 0.5, 1.5),
        "ln1_bias": centred(key_list[5], (LAYERS, C), 0.5, 3.0, (), jnp.float32),
        "qkv_w": centred(key_list[6], (LAYERS, C, 3 * C), C ** -0.5, 0.25, ((1, 4),)),
        "q_bias": centred(key_list[7], (LAYERS, C), 0.5, 3.0, (), jnp.float32),
        "v_bias": centred(key_list[8], (LAYERS, C), 0.5, 3.0, (), jnp.float32),
        "rel_table": centred(key_list[9], (LAYERS, BIAS_ROWS, HEADS), 1.0, 4.0, (), jnp.float32),
        "proj_w": centred(key_list[10], (LAYERS, C, C), (C // 32) ** -0.5, 1.5, ((1, 4),)),
        "proj_b": centred(key_list[11], (LAYERS, C), 0.5, 3.0, (), jnp.float32),
        "ln2_gain": jnp.clip(1.0 + 0.1 * jax.random.normal(key_list[12], (LAYERS, C), jnp.float32), 0.5, 1.5),
        "ln2_bias": centred(key_list[13], (LAYERS, C), 0.5, 3.0, (), jnp.float32),
        "fc1_w": centred(key_list[14], (LAYERS, C, FF), C ** -0.5, 0.25, ((1, 4),)),
        "fc1_b": centred(key_list[15], (LAYERS, FF), 0.5, 3.0, (), jnp.float32),
        "fc2_w": centred(key_list[16], (LAYERS, FF, C), FF ** -0.5, 0.125, ((1, 4),)),
        "fc2_b": centred(key_list[17], (LAYERS, C), 0.5, 3.0, (), jnp.float32),
    }


@jax.custom_vjp
def low(v):
    return lax.optimization_barrier(v.astype(jnp.bfloat16)).astype(jnp.float32)

@jax.custom_vjp
def low_back(v):
    return v

def low_keep(v):
    return (low(v), None)

def low_pass(kept, grad):
    return (grad,)

def back_keep(v):
    return (v, None)

def back_low(kept, grad):
    return (low(grad),)
low.defvjp(low_keep, low_pass)
low_back.defvjp(back_keep, back_low)
epsilon = 1e-05
highest = lax.Precision.HIGHEST

def norm_rows(values_in, norm_gain, norm_bias):
    row_mean = lax.optimization_barrier(jnp.mean(values_in, axis=-1, keepdims=True))
    centered = values_in - row_mean
    variance = lax.optimization_barrier(jnp.mean(centered * centered, axis=-1, keepdims=True))
    return centered * lax.rsqrt(variance + epsilon) * norm_gain + norm_bias

def matmul(left_side, right_side):
    return jnp.dot(left_side, right_side, precision=highest, preferred_element_type=jnp.float32)

def windows(values_in):
    blocks = SIDE // WIN
    channels = values_in.shape[-1]
    values_in = values_in.reshape(blocks, WIN, blocks, WIN, channels).transpose(0, 2, 1, 3, 4)
    return values_in.reshape(blocks * blocks, WIN2, channels)

def unwindows(values_in):
    blocks = SIDE // WIN
    channels = values_in.shape[-1]
    values_in = values_in.reshape(blocks, blocks, WIN, WIN, channels).transpose(0, 2, 1, 3, 4)
    return values_in.reshape(SIDE, SIDE, channels)

def attend(projected, table, rel_index, allowed, rolled):
    head_size = C // HEADS
    cell_grid = projected.reshape(SIDE, SIDE, 3 * C)
    if rolled:
        cell_grid = jnp.roll(cell_grid, (-SHIFT, -SHIFT), axis=(0, 1))
    window_parts = windows(cell_grid).reshape(-1, WIN2, HEADS, 3, head_size)
    queries = window_parts[:, :, :, 0]
    key_rows = window_parts[:, :, :, 1]
    values = window_parts[:, :, :, 2]
    rel_bias = jnp.transpose(table[rel_index], (2, 0, 1))
    raw_scores = jnp.einsum('wihd,wjhd->whij', queries, key_rows, precision=highest) * head_size ** (-0.5)
    raw_scores = low_back(raw_scores + rel_bias[None])
    exp_scores = jnp.exp(raw_scores) * allowed
    soft_probs = exp_scores / lax.optimization_barrier(jnp.sum(exp_scores, axis=-1, keepdims=True))
    mixed_heads = jnp.einsum('whij,wjhd->wihd', low(soft_probs), values, precision=highest)
    cell_grid = unwindows(mixed_heads.reshape(-1, WIN2, C))
    if rolled:
        cell_grid = jnp.roll(cell_grid, (SHIFT, SHIFT), axis=(0, 1))
    return cell_grid.reshape(HW, C)

def network(one_image, params, rel_index, masks):
    g1s, s1s, wqkv, qbs, vbs, tables, wproj, bproj, g2s, s2s, wfc1, bfc1, wfc2, bfc2 = params
    head_size = C // HEADS
    stream = one_image
    for layer_id in range(LAYERS):
        rolled = layer_id % 2 == 1
        q_part = qbs[layer_id].reshape(HEADS, head_size)
        qkv_shift = jnp.stack([q_part, jnp.zeros_like(q_part), vbs[layer_id].reshape(HEADS, head_size)], axis=1).reshape(3 * C)
        normed = low(norm_rows(stream, g1s[layer_id], s1s[layer_id]))
        projected = low(low_back(matmul(normed, wqkv[layer_id]) + qkv_shift))
        mixed_heads = low(low_back(attend(projected, tables[layer_id], rel_index, masks[layer_id % 2], rolled)))
        middle = stream + low_back(matmul(mixed_heads, wproj[layer_id]) + bproj[layer_id])
        second = low(norm_rows(middle, g2s[layer_id], s2s[layer_id]))
        hidden = low_back(matmul(second, wfc1[layer_id]) + bfc1[layer_id])
        active = low(jax.nn.gelu(hidden, approximate=False))
        stream = middle + low_back(matmul(active, wfc2[layer_id]) + bfc2[layer_id])
    return stream

def reference(inputs, cotangent, region_ids, rel_index, ln1_gain, ln1_bias, qkv_w, q_bias, v_bias, rel_table, proj_w, proj_b, ln2_gain, ln2_bias, fc1_w, fc1_b, fc2_w, fc2_b):
    params = tuple((item.astype(jnp.float32) for item in (ln1_gain, ln1_bias, qkv_w, q_bias, v_bias, rel_table, proj_w, proj_b, ln2_gain, ln2_bias, fc1_w, fc1_b, fc2_w, fc2_b)))
    cells = windows(region_ids.reshape(SIDE, SIDE, 1)).reshape(-1, WIN2)
    shifted_mask = (cells[:, :, None] == cells[:, None, :]).astype(jnp.float32)[:, None]
    masks = (jnp.ones_like(shifted_mask), shifted_mask)

    def one_step(grad_sums, item_pair):
        picture, upstream = item_pair

        def forward_fn(stream, prm):
            return network(stream, prm, rel_index, masks)
        result, pullback = jax.vjp(forward_fn, picture.astype(jnp.float32), params)
        grad_picture, grad_params = pullback(upstream.astype(jnp.float32))
        grad_sums = jax.tree.map(jnp.add, grad_sums, grad_params)
        return (grad_sums, (result, grad_picture))
    zero_grads = jax.tree.map(jnp.zeros_like, params)
    grads, (result, grad_inputs) = lax.scan(one_step, zero_grads, (inputs, cotangent))
    return (result, grad_inputs) + tuple(grads)
```

```python
import functools

import jax
import jax.numpy as jnp
from jax import lax
from jax.experimental import pallas as pl
from jax.experimental.pallas import tpu as pltpu
from jax.sharding import PartitionSpec as P

C = 512
HEADS = 16
HEAD = 32
FF = 2048
WIN = 7
SHIFT = 3
WIN2 = 49
BIAS_ROWS = 169
SIDE = 56
LAYERS = 2

BAND = WIN * SIDE
WPB = SIDE // WIN
PAD = 64
WROWS = WPB * PAD
GROUPS = 4
SCORES = HEADS * PAD
HALO = SHIFT * SIDE
CHUNK = 512

EPS = 1e-05
LOG2E = 1.4426950408889634
SCALE = HEAD**-0.5
NEG = -1e30
F32 = jnp.float32
BF16 = jnp.bfloat16
highest = lax.Precision.HIGHEST


def dot(left, right):
    return lax.dot_general(left, right, (((1,), (0,)), ((), ())), preferred_element_type=F32)


def dot_t(left, right):
    return lax.dot_general(left, right, (((1,), (1,)), ((), ())), preferred_element_type=F32)


def dot_tn(left, right):
    return lax.dot_general(left, right, (((0,), (0,)), ((), ())), preferred_element_type=F32)


def normalize(values):
    mean = jnp.mean(values, axis=-1, keepdims=True)
    centered = values - mean
    var = jnp.mean(centered * centered, axis=-1, keepdims=True)
    inv = lax.rsqrt(var + EPS)
    return centered * inv, inv


def head_masks():
    lane = lax.broadcasted_iota(jnp.int32, (PAD, 128), 1)
    return [((lane >> 5) == h).astype(F32).astype(BF16) for h in range(4)]


def spread(values, masks):
    return jnp.concatenate([values * m for m in masks], axis=0)


def group_sum_weights():
    row = lax.broadcasted_iota(jnp.int32, (4 * PAD, 4 * PAD), 0) >> 6
    col = lax.broadcasted_iota(jnp.int32, (4 * PAD, 4 * PAD), 1) >> 6
    return (row == col).astype(F32).astype(BF16)


def row_valid():
    row = lax.broadcasted_iota(jnp.int32, (WROWS, 1), 0) & (PAD - 1)
    return (row < WIN2).astype(F32)


def attn_fwd_kernel(rolled, *refs):
    if rolled:
        (x_ref, g_ref, s_ref, wqkv_ref, qkvb_ref, perm_ref, permt_ref, bias_ref, mask_ref,
         wproj_ref, pb_ref, proj_ref, p_ref, att_ref, m_ref, attw) = refs
    else:
        (x_ref, g_ref, s_ref, wqkv_ref, qkvb_ref, perm_ref, permt_ref, bias_ref,
         wproj_ref, pb_ref, proj_ref, p_ref, att_ref, m_ref, attw) = refs
        mask_ref = None
    x = x_ref[...].astype(F32)
    xhat, _ = normalize(x)
    a = (xhat * g_ref[...] + s_ref[...]).astype(BF16)
    aw = dot(perm_ref[...], a).astype(BF16)
    valid = row_valid()
    for c in range(3):
        cols = slice(c * C, (c + 1) * C)
        y = dot(aw, wqkv_ref[:, cols]) + qkvb_ref[:, cols] * valid
        proj_ref[:, cols] = y.astype(BF16)
    masks = head_masks()
    sums = group_sum_weights()

    def one_window(w):
        rows = pl.ds(pl.multiple_of(w * PAD, PAD), PAD)
        eb = []
        for g in range(GROUPS):
            q = proj_ref[rows, 128 * g : 128 * g + 128]
            k = proj_ref[rows, C + 128 * g : C + 128 * g + 128]
            t = dot_t(q, spread(k, masks)) * (SCALE * LOG2E) + bias_ref[:, 256 * g : 256 * g + 256]
            if mask_ref is not None:
                t = t + mask_ref[w]
            eb.append(jnp.exp2(t).astype(BF16))
        total = dot(jnp.concatenate(eb, axis=0), sums)
        for g in range(GROUPS):
            p = (eb[g].astype(F32) / total[PAD * g : PAD * g + PAD]).astype(BF16)
            p_ref[rows, 256 * g : 256 * g + 256] = p
            v = proj_ref[rows, 2 * C + 128 * g : 2 * C + 128 * g + 128]
            attw[rows, 128 * g : 128 * g + 128] = dot(p, spread(v, masks)).astype(BF16)

    def pair(i, carry):
        one_window(2 * i)
        one_window(2 * i + 1)
        return carry

    lax.fori_loop(0, WPB // 2, pair, 0)
    att = dot(permt_ref[...], attw[...]).astype(BF16)
    att_ref[...] = att
    m_ref[...] = x + (dot(att, wproj_ref[...]) + pb_ref[...])


def mlp_fwd_kernel(m_ref, g_ref, s_ref, w1_ref, b1_ref, w2_ref, b2_ref, act_ref, slope_ref, h_ref):
    m = m_ref[...]
    xhat, _ = normalize(m)
    b = (xhat * g_ref[...] + s_ref[...]).astype(BF16)
    acc = m + b2_ref[...]
    for c in range(FF // CHUNK):
        cols = slice(c * CHUNK, (c + 1) * CHUNK)
        u = dot(b, w1_ref[:, cols]) + b1_ref[:, cols]
        cdf = 0.5 + 0.5 * lax.erf(u * (0.5**0.5))
        pdf = jnp.exp2(u * u * (-0.5 * LOG2E)) * 0.3989422804014327
        act = (u * cdf).astype(BF16)
        act_ref[:, cols] = act
        slope_ref[:, cols] = (cdf + u * pdf).astype(BF16)
        acc = acc + dot(act, w2_ref[cols, :])
    h_ref[...] = acc


def first_step():
    return pl.program_id(0) == 0


def accumulate(ref, value):
    @pl.when(first_step())
    def _():
        ref[...] = value

    @pl.when(jnp.logical_not(first_step()))
    def _():
        ref[...] += value


def col_sum(values):
    return jnp.sum(values, axis=0, keepdims=True)


def norm_back(e, xhat, inv, gain):
    eg = e * gain
    mean1 = jnp.mean(eg, axis=-1, keepdims=True)
    mean2 = jnp.mean(eg * xhat, axis=-1, keepdims=True)
    return inv * (eg - mean1 - xhat * mean2)


def mlp_bwd_kernel(split, dh_ref, m_ref, act_ref, slope_ref, g_ref, s_ref, w1_ref, w2_ref,
                   dm_ref, gw1_ref, gw2_ref, gb1_ref, gb2_ref, gg_ref, gs_ref, acc1, acc2):
    dh = dh_ref[...].astype(F32)
    dz = dh.astype(BF16)
    accumulate(gb2_ref, col_sum(dz.astype(F32)))
    xhat, inv = normalize(m_ref[...])
    b = (xhat * g_ref[...] + s_ref[...]).astype(BF16)
    e = jnp.zeros((BAND, C), F32)

    @pl.when(first_step())
    def _():
        acc1[...] = jnp.zeros_like(acc1)
        acc2[...] = jnp.zeros_like(acc2)
        gb1_ref[...] = jnp.zeros_like(gb1_ref)

    for c in range(FF // CHUNK):
        cols = slice(c * CHUNK, (c + 1) * CHUNK)
        dg = dot_t(dz, w2_ref[cols, :])
        du = (dg * slope_ref[:, cols].astype(F32)).astype(BF16)
        gb1_ref[:, cols] += col_sum(du.astype(F32))
        acc2[:, cols] += dot_tn(dz, act_ref[:, cols])
        acc1[:, cols] += dot_tn(b, du)
        e = e + dot_t(du, w1_ref[:, cols])
    accumulate(gg_ref, col_sum(e * xhat))
    accumulate(gs_ref, col_sum(e))
    dm_ref[...] = dh + norm_back(e, xhat, inv, g_ref[...])

    @pl.when(pl.program_id(0) == pl.num_programs(0) - 1)
    def _():
        write_split(gw1_ref, acc1[...].astype(BF16), split)
        for c in range(FF // CHUNK):
            cols = slice(c * CHUNK, (c + 1) * CHUNK)
            gw2_ref[cols, :] = jnp.transpose(acc2[:, cols]).astype(BF16)


def write_split(ref, value, split):
    ref[...] = value


def attn_bwd_kernel(split, dm_ref, x_ref, att_ref, proj_ref, p_ref, g_ref, s_ref, wqkv_ref,
                    wproj_ref, perm_ref, permt_ref,
                    dx_ref, gwqkv_ref, gwproj_ref, gqkvb_ref, gpb_ref, gg_ref, gs_ref, gbias_ref,
                    accq, accp, dattw, attw, dqw, dkt, dvt):
    dm = dm_ref[...]
    dy = dm.astype(BF16)
    att = att_ref[...]
    accumulate(gpb_ref, col_sum(dy.astype(F32)))
    accumulate(accp, dot_tn(att, dy))
    datt = dot_t(dy, wproj_ref[...]).astype(BF16)
    dattw[...] = dot(perm_ref[...], datt).astype(BF16)
    attw[...] = dot(perm_ref[...], att).astype(BF16)

    @pl.when(first_step())
    def _():
        gbias_ref[...] = jnp.zeros_like(gbias_ref)

    masks = head_masks()
    ones = jnp.concatenate(masks, axis=0)
    low_half = lax.broadcasted_iota(jnp.int32, (HEAD, 128), 1) < PAD

    def one_window(w):
        rows = pl.ds(pl.multiple_of(w * PAD, PAD), PAD)
        dks, dvs = [], []
        for g in range(GROUPS):
            lanes = slice(128 * g, 128 * g + 128)
            wide = slice(256 * g, 256 * g + 256)
            q = proj_ref[rows, lanes]
            k = proj_ref[rows, C + 128 * g : C + 128 * g + 128]
            v = proj_ref[rows, 2 * C + 128 * g : 2 * C + 128 * g + 128]
            p = p_ref[rows, wide]
            da = dattw[rows, lanes]
            inner = (-(da.astype(F32) * attw[rows, lanes].astype(F32))).astype(BF16)
            left = jnp.concatenate([da, inner], axis=1)
            right = jnp.concatenate([spread(v, masks), ones], axis=1)
            ds = (p.astype(F32) * dot_t(left, right)).astype(BF16)
            gbias_ref[:, wide] += ds.astype(F32)
            dqw[rows, lanes] = (dot(ds, spread(k, masks)) * SCALE).astype(BF16)
            dks.append(dot_tn(q, ds))
            dvs.append(dot_tn(da, p))
        return dks, dvs

    def diagonal(first, second):
        parts = []
        for h in range(4):
            lanes = slice(128 * (h // 2), 128 * (h // 2) + 128)
            one = first[HEAD * h : HEAD * h + HEAD, lanes]
            two = second[HEAD * h : HEAD * h + HEAD, lanes]
            if h % 2 == 0:
                two = pltpu.roll(two, PAD, 1)
            else:
                one = pltpu.roll(one, PAD, 1)
            parts.append(jnp.where(low_half, one, two))
        return jnp.concatenate(parts, axis=0)

    def pair(i, carry):
        dk0, dv0 = one_window(2 * i)
        dk1, dv1 = one_window(2 * i + 1)
        cols = pl.ds(pl.multiple_of(i * 128, 128), 128)
        for g in range(GROUPS):
            dkt[128 * g : 128 * g + 128, cols] = (diagonal(dk0[g], dk1[g]) * SCALE).astype(BF16)
            dvt[128 * g : 128 * g + 128, cols] = diagonal(dv0[g], dv1[g]).astype(BF16)
        return carry

    lax.fori_loop(0, WPB // 2, pair, 0)
    permt = permt_ref[...]
    x = x_ref[...].astype(F32)
    xhat, inv = normalize(x)
    a = (xhat * g_ref[...] + s_ref[...]).astype(BF16)
    e = jnp.zeros((BAND, C), F32)

    @pl.when(first_step())
    def _():
        accq[...] = jnp.zeros_like(accq)
        gqkvb_ref[...] = jnp.zeros_like(gqkvb_ref)

    for c in range(3):
        cols = slice(c * C, (c + 1) * C)
        if c == 0:
            dp = dot(permt, dqw[...])
        else:
            dp = dot_t(permt, (dkt if c == 1 else dvt)[...])
        gqkvb_ref[:, cols] += col_sum(dp)
        dp = dp.astype(BF16)
        accq[:, cols] += dot_tn(a, dp)
        e = e + dot_t(dp, wqkv_ref[:, cols])
    accumulate(gg_ref, col_sum(e * xhat))
    accumulate(gs_ref, col_sum(e))
    dx_ref[...] = dm + norm_back(e, xhat, inv, g_ref[...])

    @pl.when(pl.program_id(0) == pl.num_programs(0) - 1)
    def _():
        write_split(gwqkv_ref, accq[...].astype(BF16), split)
        write_split(gwproj_ref, accp[...].astype(BF16), split)


def band_spec(*shape):
    return pl.BlockSpec((None,) + shape, lambda i: (i,) + (0,) * len(shape))


def whole_spec(*shape):
    return pl.BlockSpec(shape, lambda i: (0,) * len(shape))


def params():
    return pltpu.CompilerParams(vmem_limit_bytes=60 << 20)


def cost(flops, bytes_accessed, transcendentals=0):
    return pl.CostEstimate(
        flops=int(flops), bytes_accessed=int(bytes_accessed), transcendentals=int(transcendentals)
    )


def shape(*dims, dtype=F32):
    return jax.ShapeDtypeStruct(dims, dtype)


def attn_fwd(x, gain, shift, wqkv, qkvb, perm, permt, bias, mask, wproj, pb):
    n = x.shape[0]
    rolled = mask is not None
    in_specs = [
        band_spec(BAND, C), whole_spec(1, C), whole_spec(1, C), whole_spec(C, 3 * C),
        whole_spec(1, 3 * C), whole_spec(WROWS, BAND), whole_spec(BAND, WROWS),
        whole_spec(PAD, SCORES),
    ]
    args = [x, gain, shift, wqkv, qkvb, perm, permt, bias]
    if rolled:
        kinds = mask.shape[0]
        in_specs.append(pl.BlockSpec((None, WPB, PAD, 256), lambda i: (i % kinds, 0, 0, 0)))
        args.append(mask)
    in_specs += [whole_spec(C, C), whole_spec(1, C)]
    args += [wproj, pb]
    return pl.pallas_call(
        functools.partial(attn_fwd_kernel, rolled),
        grid=(n,),
        in_specs=in_specs,
        out_specs=[band_spec(WROWS, 3 * C), band_spec(WROWS, SCORES), band_spec(BAND, C),
                   band_spec(BAND, C)],
        out_shape=[shape(n, WROWS, 3 * C, dtype=BF16), shape(n, WROWS, SCORES, dtype=BF16),
                   shape(n, BAND, C, dtype=BF16), shape(n, BAND, C)],
        scratch_shapes=[pltpu.VMEM((WROWS, C), BF16)],
        compiler_params=params(),
        cost_estimate=cost(n * 6e9, n * 5e6, n * 5e5),
        name="attn_fwd",
    )(*args)


def mlp_fwd(m, gain, shift, w1, b1, w2, b2):
    n = m.shape[0]
    return pl.pallas_call(
        mlp_fwd_kernel,
        grid=(n,),
        in_specs=[band_spec(BAND, C), whole_spec(1, C), whole_spec(1, C), whole_spec(C, FF),
                  whole_spec(1, FF), whole_spec(FF, C), whole_spec(1, C)],
        out_specs=[band_spec(BAND, FF), band_spec(BAND, FF), band_spec(BAND, C)],
        out_shape=[shape(n, BAND, FF, dtype=BF16), shape(n, BAND, FF, dtype=BF16),
                   shape(n, BAND, C)],
        compiler_params=params(),
        cost_estimate=cost(n * 6e9, n * 5e6, n * 16e5),
        name="mlp_fwd",
    )(m, gain, shift, w1, b1, w2, b2)


def mlp_bwd(split, dh, m, act, slope, gain, shift, w1, w2):
    n = m.shape[0]
    return pl.pallas_call(
        functools.partial(mlp_bwd_kernel, split),
        grid=(n,),
        in_specs=[band_spec(BAND, C), band_spec(BAND, C), band_spec(BAND, FF), band_spec(BAND, FF),
                  whole_spec(1, C), whole_spec(1, C), whole_spec(C, FF), whole_spec(FF, C)],
        out_specs=[band_spec(BAND, C), whole_spec(C, FF), whole_spec(FF, C), whole_spec(1, FF),
                   whole_spec(1, C), whole_spec(1, C), whole_spec(1, C)],
        out_shape=[shape(n, BAND, C), shape(C, FF, dtype=BF16), shape(FF, C, dtype=BF16),
                   shape(1, FF), shape(1, C), shape(1, C), shape(1, C)],
        scratch_shapes=[pltpu.VMEM((C, FF), F32), pltpu.VMEM((C, FF), F32)],
        compiler_params=params(),
        cost_estimate=cost(n * 12e9, n * 6e6),
        name="mlp_bwd",
    )(dh, m, act, slope, gain, shift, w1, w2)


def attn_bwd(split, dm, x, att, proj, p, gain, shift, wqkv, wproj, perm, permt):
    n = dm.shape[0]
    return pl.pallas_call(
        functools.partial(attn_bwd_kernel, split),
        grid=(n,),
        in_specs=[band_spec(BAND, C), band_spec(BAND, C), band_spec(BAND, C),
                  band_spec(WROWS, 3 * C), band_spec(WROWS, SCORES), whole_spec(1, C),
                  whole_spec(1, C), whole_spec(C, 3 * C), whole_spec(C, C),
                  whole_spec(WROWS, BAND), whole_spec(BAND, WROWS)],
        out_specs=[band_spec(BAND, C), whole_spec(C, 3 * C), whole_spec(C, C),
                   whole_spec(1, 3 * C), whole_spec(1, C), whole_spec(1, C), whole_spec(1, C),
                   whole_spec(PAD, SCORES)],
        out_shape=[shape(n, BAND, C), shape(C, 3 * C, dtype=BF16), shape(C, C, dtype=BF16),
                   shape(1, 3 * C), shape(1, C), shape(1, C), shape(1, C), shape(PAD, SCORES)],
        scratch_shapes=[pltpu.VMEM((C, 3 * C), F32), pltpu.VMEM((C, C), F32),
                        pltpu.VMEM((WROWS, C), BF16), pltpu.VMEM((WROWS, C), BF16),
                        pltpu.VMEM((WROWS, C), BF16), pltpu.VMEM((C, WROWS), BF16),
                        pltpu.VMEM((C, WROWS), BF16)],
        compiler_params=params(),
        cost_estimate=cost(n * 10e9, n * 6e6),
        name="attn_bwd",
    )(dm, x, att, proj, p, gain, shift, wqkv, wproj, perm, permt)


def window_permutation(rolled):
    row = jnp.arange(WROWS, dtype=jnp.int32)
    window, cell = row // PAD, row % PAD
    col = window * WIN + cell % WIN
    if rolled:
        col = (col + SHIFT) % SIDE
    source = jnp.where(cell < WIN2, cell // WIN * SIDE + col, -1)
    token = jnp.arange(BAND, dtype=jnp.int32)
    perm = (source[:, None] == token[None, :]).astype(BF16)
    permt = (source[None, :] == token[:, None]).astype(BF16)
    return perm, permt


def padded_selector(rel_index):
    index = jnp.full((PAD, PAD), -1, jnp.int32).at[:WIN2, :WIN2].set(rel_index)
    return (index[:, :, None] == jnp.arange(BIAS_ROWS, dtype=jnp.int32)).astype(F32)


def score_bias(selector, table):
    bias = jnp.einsum("ijr,rh->ihj", selector, table, precision=highest) * LOG2E
    real = (jnp.arange(PAD) < WIN2)[None, None, :]
    return jnp.where(real, bias, NEG).reshape(PAD, SCORES)


def table_grad(selector, grad_bias):
    return jnp.einsum(
        "ijr,ihj->rh", selector, grad_bias.reshape(PAD, HEADS, PAD), precision=highest
    )


def score_mask(region_rows):
    rows = region_rows.shape[0]
    ids = region_rows.reshape(rows // WIN, WIN, WPB, WIN).transpose(0, 2, 1, 3)
    ids = ids.reshape(rows // WIN, WPB, WIN2)
    ids = jnp.pad(ids, ((0, 0), (0, 0), (0, PAD - WIN2)), constant_values=-1)
    real = jnp.arange(PAD) < WIN2
    blocked = (ids[..., :, None] != ids[..., None, :]) & real[:, None]
    mask = jnp.where(blocked, NEG, 0.0).astype(F32)
    return jnp.concatenate([mask] * 4, axis=-1)


def partner(block, bit):
    count = lax.axis_size("seq")
    return lax.ppermute(block, "seq", [(i, i ^ (1 << bit)) for i in range(count)])


def from_behind(block, distance):
    count = lax.axis_size("seq")
    return lax.ppermute(block, "seq", [((i - distance) % count, i) for i in range(count)])


def group_exchange(pieces):
    count = pieces.shape[0]
    position = lax.axis_index("seq")
    for bit in range(count.bit_length() - 1):
        flag = position // (1 << bit) % 2 == 1
        shaped = pieces.reshape((count // (2 << bit), 2, 1 << bit) + pieces.shape[1:])
        lower, upper = shaped[:, 0], shaped[:, 1]
        kept = jnp.where(flag, upper, lower)
        incoming = partner(jnp.where(flag, lower, upper).astype(BF16), bit).astype(pieces.dtype)
        first = jnp.where(flag, incoming, kept)
        second = jnp.where(flag, kept, incoming)
        pieces = jnp.stack([first, second], axis=1).reshape(pieces.shape)
    return pieces


def gather_rows(shard):
    count = lax.axis_size("seq")
    rows = shard.shape[0] // count
    mine = lax.dynamic_slice_in_dim(shard, lax.axis_index("seq") * rows, rows, 0)
    return lax.all_gather(mine, ("fsdp", "seq"), axis=0, tiled=True)


def scatter_rows(grad):
    seq, fsdp = lax.axis_size("seq"), lax.axis_size("fsdp")
    rows, cols = grad.shape
    part = rows // (seq * fsdp)
    grad = grad.reshape(fsdp, seq, part, cols).transpose(1, 0, 2, 3).reshape(rows, cols)
    grad = lax.psum_scatter(grad, "seq", scatter_dimension=0, tiled=True)
    grad = lax.psum_scatter(grad, "fsdp", scatter_dimension=0, tiled=True)
    return lax.all_gather(grad, "seq", axis=0, tiled=True).astype(F32)


def split_heads(w):
    return w.reshape(w.shape[0], HEADS, 3, HEAD).transpose(0, 2, 1, 3).reshape(w.shape)


def join_heads(w):
    return w.reshape(w.shape[0], 3, HEADS, HEAD).transpose(0, 2, 1, 3).reshape(w.shape)


def on_device(inputs, cotangent, region_ids, rel_index, ln1_gain, ln1_bias, qkv_w, q_bias, v_bias,
              rel_table, proj_w, proj_b, ln2_gain, ln2_bias, fc1_w, fc1_b, fc2_w, fc2_b):
    images, tokens, features = inputs.shape
    position = lax.axis_index("seq")
    group = 1
    while group * tokens % BAND:
        group *= 2
    per_group = images // group
    local = group * tokens
    bands = local // BAND

    def regroup(x):
        if group == 1:
            return x
        x = group_exchange(x.reshape(group, per_group, tokens, features))
        return x.transpose(1, 0, 2, 3).reshape(per_group, local, features)

    def ungroup(x):
        if group == 1:
            return x
        x = x.reshape(per_group, group, tokens, features).transpose(1, 0, 2, 3)
        return group_exchange(x).reshape(images, tokens, features)

    def roll_in(x):
        tail = from_behind(x[:, :HALO].astype(BF16), -group).astype(x.dtype)
        return jnp.concatenate([x[:, HALO:], tail], axis=1)

    def roll_out(x):
        head = from_behind(x[:, -HALO:].astype(BF16), group).astype(x.dtype)
        return jnp.concatenate([head, x[:, :-HALO]], axis=1)

    def as_bands(x):
        return x.reshape(per_group * bands, BAND, features)

    def as_images(x):
        return x.reshape(per_group, local, features)

    wqkv = [gather_rows(split_heads(qkv_w[l])) for l in range(LAYERS)]
    wproj = [gather_rows(proj_w[l]) for l in range(LAYERS)]
    wfc1 = [gather_rows(fc1_w[l]) for l in range(LAYERS)]
    wfc2 = [gather_rows(fc2_w[l]) for l in range(LAYERS)]

    selector = padded_selector(rel_index)
    region_rows = lax.dynamic_slice_in_dim(
        region_ids, position // group * bands * WIN, bands * WIN, 0
    )
    masks = (None, score_mask(region_rows))
    perms = (window_permutation(False), window_permutation(True))

    stream = regroup(inputs)
    upstream = roll_in(regroup(cotangent))
    saved = []
    for l in range(LAYERS):
        kind = l % 2
        if l > 0:
            stream = roll_in(stream) if kind else roll_out(stream)
        x = as_bands(stream)
        qkvb = jnp.concatenate([q_bias[l], jnp.zeros_like(q_bias[l]), v_bias[l]])[None]
        bias = score_bias(selector, rel_table[l])
        proj, p, att, m = attn_fwd(
            x, ln1_gain[l][None], ln1_bias[l][None], wqkv[l], qkvb, *perms[kind], bias,
            masks[kind], wproj[l], proj_b[l][None],
        )
        act, slope, h = mlp_fwd(
            m, ln2_gain[l][None], ln2_bias[l][None], wfc1[l], fc1_b[l][None], wfc2[l],
            fc2_b[l][None],
        )
        saved.append((x, proj, p, att, m, act, slope))
        stream = as_images(h)
    out = ungroup(roll_out(stream))

    big, small = [], []
    for l in reversed(range(LAYERS)):
        kind = l % 2
        x, proj, p, att, m, act, slope = saved[l]
        dm, gw1, gw2, gb1, gb2, gg2, gs2 = mlp_bwd(
            None, as_bands(upstream), m, act, slope, ln2_gain[l][None], ln2_bias[l][None],
            wfc1[l], wfc2[l],
        )
        dx, gwqkv, gwproj, gqkvb, gpb, gg1, gs1, gbias = attn_bwd(
            None, dm, x, att, proj, p, ln1_gain[l][None], ln1_bias[l][None], wqkv[l], wproj[l],
            *perms[kind],
        )
        upstream = as_images(dx)
        if l > 0:
            upstream = roll_out(upstream) if kind else roll_in(upstream)
        big.insert(0, (
            join_heads(scatter_rows(gwqkv)), scatter_rows(gwproj), scatter_rows(gw1),
            scatter_rows(gw2),
        ))
        small.insert(0, (
            gg1[0], gs1[0], gqkvb[0, :C], gqkvb[0, 2 * C :], table_grad(selector, gbias),
            gpb[0], gg2[0], gs2[0], gb1[0], gb2[0],
        ))
    grad_in = ungroup(upstream)
    small = lax.psum(
        tuple(jnp.stack([layer[i] for layer in small]) for i in range(10)), ("seq", "fsdp")
    )
    big = [jnp.stack([layer[i] for layer in big]) for i in range(4)]
    return (
        out, grad_in, small[0], small[1], big[0], small[2], small[3], small[4], big[1], small[5],
        small[6], small[7], big[2], small[8], big[3], small[9],
    )


def solution(mesh):
    tokens = P("fsdp", "seq", None)
    matrix = P(None, "fsdp", None)
    in_specs = (
        tokens, tokens, P(), P(), P(), P(), matrix, P(), P(), P(), matrix, P(), P(), P(), matrix,
        P(), matrix, P(),
    )
    out_specs = (
        tokens, tokens, P(), P(), matrix, P(), P(), P(), matrix, P(), P(), P(), matrix, P(),
        matrix, P(),
    )
    return jax.shard_map(
        on_device, mesh=mesh, in_specs=in_specs, out_specs=out_specs, check_vma=False
    )
```

```python
import functools

import jax
import jax.numpy as jnp
from jax import lax
from jax.experimental import pallas as pl
from jax.experimental.pallas import tpu as pltpu
from jax.sharding import PartitionSpec as P

C = 512
HEADS = 16
HEAD = 32
FF = 2048
WIN = 7
SHIFT = 3
WIN2 = 49
BIAS_ROWS = 169
SIDE = 56
LAYERS = 2

BAND = WIN * SIDE
WPB = SIDE // WIN
PAD = 64
WROWS = WPB * PAD
GROUPS = 4
SCORES = HEADS * PAD
HALO = SHIFT * SIDE
CHUNK = 512

EPS = 1e-05
LOG2E = 1.4426950408889634
SCALE = HEAD**-0.5
NEG = -1e30
F32 = jnp.float32
BF16 = jnp.bfloat16
highest = lax.Precision.HIGHEST


def dot(left, right):
    return lax.dot_general(left, right, (((1,), (0,)), ((), ())), preferred_element_type=F32)


def dot_t(left, right):
    return lax.dot_general(left, right, (((1,), (1,)), ((), ())), preferred_element_type=F32)


def dot_tn(left, right):
    return lax.dot_general(left, right, (((0,), (0,)), ((), ())), preferred_element_type=F32)


def normalize(values):
    mean = jnp.mean(values, axis=-1, keepdims=True)
    centered = values - mean
    var = jnp.mean(centered * centered, axis=-1, keepdims=True)
    inv = lax.rsqrt(var + EPS)
    return centered * inv, inv


def head_masks():
    lane = lax.broadcasted_iota(jnp.int32, (PAD, 128), 1)
    return [((lane >> 5) == h).astype(F32).astype(BF16) for h in range(4)]


def spread(values, masks):
    return jnp.concatenate([values * m for m in masks], axis=0)


def group_sum_weights():
    row = lax.broadcasted_iota(jnp.int32, (4 * PAD, 4 * PAD), 0) >> 6
    col = lax.broadcasted_iota(jnp.int32, (4 * PAD, 4 * PAD), 1) >> 6
    return (row == col).astype(F32).astype(BF16)


def row_valid():
    row = lax.broadcasted_iota(jnp.int32, (WROWS, 1), 0) & (PAD - 1)
    return (row < WIN2).astype(F32)


def first_step():
    return pl.program_id(0) == 0


def last_step():
    return pl.program_id(0) == pl.num_programs(0) - 1


def fetch_weights(sizes, places, own_ref, other_ref, sems):
    seq, fsdp = sizes
    me = lax.axis_index("seq")
    plane, core, line = me // 2, me % 2, lax.axis_index("fsdp")
    copies = []
    for source, side in ((own_ref, core), (other_ref, 1 - core)):
        for d in range(seq // 2):
            s = (plane ^ d) * 2 + side
            for e in range(fsdp):
                for k, place in enumerate(places):
                    copies.append(pltpu.make_async_copy(
                        source.at[d, e, k], place(s, line ^ e), sems.at[len(copies)]
                    ))
    for copy in copies:
        copy.start()
    for copy in copies:
        copy.wait()


def aligned(start, size):
    return pl.ds(pl.multiple_of(start, size), size)


def by_columns(sizes, ref):
    seq, fsdp = sizes
    rows, cols = C // fsdp, FF // seq
    return lambda s, z: ref.at[aligned(z * rows, rows), aligned(s * cols, cols)]


def by_blocks(sizes, ref):
    seq, fsdp = sizes
    rows, cols, across = C // fsdp, FF // seq, seq // 4

    def place(s, z):
        row = z * (FF // fsdp) + s // across * rows
        return ref.at[aligned(row, rows), aligned(s % across * cols, cols)]

    return place


def attn_fwd_kernel(sizes, rolled, *refs):
    if rolled:
        (x_ref, g_ref, s_ref, own_ref, other_ref, qkvb_ref, perm_ref, permt_ref, bias_ref,
         mask_ref, pb_ref, proj_ref, p_ref, att_ref, m_ref, attw, w_ref, sems) = refs
    else:
        (x_ref, g_ref, s_ref, own_ref, other_ref, qkvb_ref, perm_ref, permt_ref, bias_ref,
         pb_ref, proj_ref, p_ref, att_ref, m_ref, attw, w_ref, sems) = refs
        mask_ref = None

    @pl.when(first_step())
    def _():
        fetch_weights(sizes, [by_columns(sizes, w_ref)], own_ref, other_ref, sems)

    x = x_ref[...].astype(F32)
    xhat, _ = normalize(x)
    a = (xhat * g_ref[...] + s_ref[...]).astype(BF16)
    aw = dot(perm_ref[...], a).astype(BF16)
    valid = row_valid()
    for c in range(3):
        cols = slice(c * C, (c + 1) * C)
        y = dot(aw, w_ref[:, cols]) + qkvb_ref[:, cols] * valid
        proj_ref[:, cols] = y.astype(BF16)
    masks = head_masks()
    sums = group_sum_weights()

    def one_window(w):
        rows = pl.ds(pl.multiple_of(w * PAD, PAD), PAD)
        eb = []
        for g in range(GROUPS):
            q = proj_ref[rows, 128 * g : 128 * g + 128]
            k = proj_ref[rows, C + 128 * g : C + 128 * g + 128]
            t = dot_t(q, spread(k, masks)) * (SCALE * LOG2E) + bias_ref[:, 256 * g : 256 * g + 256]
            if mask_ref is not None:
                t = t + mask_ref[w]
            eb.append(jnp.exp2(t).astype(BF16))
        total = dot(jnp.concatenate(eb, axis=0), sums)
        for g in range(GROUPS):
            p = (eb[g].astype(F32) / total[PAD * g : PAD * g + PAD]).astype(BF16)
            p_ref[rows, 256 * g : 256 * g + 256] = p
            v = proj_ref[rows, 2 * C + 128 * g : 2 * C + 128 * g + 128]
            attw[rows, 128 * g : 128 * g + 128] = dot(p, spread(v, masks)).astype(BF16)

    def pair(i, carry):
        one_window(2 * i)
        one_window(2 * i + 1)
        return carry

    lax.fori_loop(0, WPB // 2, pair, 0)
    att = dot(permt_ref[...], attw[...]).astype(BF16)
    att_ref[...] = att
    m_ref[...] = x + (dot(att, w_ref[:, 3 * C :]) + pb_ref[...])


def mlp_fwd_kernel(sizes, m_ref, g_ref, s_ref, own_ref, other_ref, b1_ref, b2_ref,
                   act_ref, slope_ref, h_ref, w1_ref, w2_ref, sems):
    @pl.when(first_step())
    def _():
        places = [by_columns(sizes, w1_ref), by_blocks(sizes, w2_ref)]
        fetch_weights(sizes, places, own_ref, other_ref, sems)

    m = m_ref[...]
    xhat, _ = normalize(m)
    b = (xhat * g_ref[...] + s_ref[...]).astype(BF16)
    acc = m + b2_ref[...]
    for c in range(FF // CHUNK):
        cols = slice(c * CHUNK, (c + 1) * CHUNK)
        u = dot(b, w1_ref[:, cols]) + b1_ref[:, cols]
        cdf = 0.5 + 0.5 * lax.erf(u * (0.5**0.5))
        pdf = jnp.exp2(u * u * (-0.5 * LOG2E)) * 0.3989422804014327
        act = (u * cdf).astype(BF16)
        act_ref[:, cols] = act
        slope_ref[:, cols] = (cdf + u * pdf).astype(BF16)
        acc = acc + dot(act, w2_ref[cols, :])
    h_ref[...] = acc


def accumulate(ref, value):
    @pl.when(first_step())
    def _():
        ref[...] = value

    @pl.when(jnp.logical_not(first_step()))
    def _():
        ref[...] += value


def col_sum(values):
    return jnp.sum(values, axis=0, keepdims=True)


def norm_back(e, xhat, inv, gain):
    eg = e * gain
    mean1 = jnp.mean(eg, axis=-1, keepdims=True)
    mean2 = jnp.mean(eg * xhat, axis=-1, keepdims=True)
    return inv * (eg - mean1 - xhat * mean2)


def mlp_bwd_kernel(sizes, dh_ref, m_ref, act_ref, slope_ref, g_ref, s_ref, own_ref, other_ref,
                   dm_ref, gw_ref, gb1_ref, gb2_ref, gg_ref, gs_ref, acc1, acc2, w1_ref, w2_ref,
                   sems):
    @pl.when(first_step())
    def _():
        places = [by_columns(sizes, w1_ref), by_blocks(sizes, w2_ref)]
        fetch_weights(sizes, places, own_ref, other_ref, sems)

    dh = dh_ref[...].astype(F32)
    dz = dh.astype(BF16)
    accumulate(gb2_ref, col_sum(dz.astype(F32)))
    xhat, inv = normalize(m_ref[...])
    b = (xhat * g_ref[...] + s_ref[...]).astype(BF16)
    e = jnp.zeros((BAND, C), F32)

    @pl.when(first_step())
    def _():
        acc1[...] = jnp.zeros_like(acc1)
        acc2[...] = jnp.zeros_like(acc2)
        gb1_ref[...] = jnp.zeros_like(gb1_ref)

    for c in range(FF // CHUNK):
        cols = slice(c * CHUNK, (c + 1) * CHUNK)
        dg = dot_t(dz, w2_ref[cols, :])
        du = (dg * slope_ref[:, cols].astype(F32)).astype(BF16)
        gb1_ref[:, cols] += col_sum(du.astype(F32))
        acc2[:, cols] += dot_tn(dz, act_ref[:, cols])
        acc1[:, cols] += dot_tn(b, du)
        e = e + dot_t(du, w1_ref[:, cols])
    accumulate(gg_ref, col_sum(e * xhat))
    accumulate(gs_ref, col_sum(e))
    dm_ref[...] = dh + norm_back(e, xhat, inv, g_ref[...])

    @pl.when(last_step())
    def _():
        write_pieces(sizes, gw_ref, 0, acc1)
        seq, fsdp = sizes
        rows, cols, across = C // fsdp, FF // seq, seq // fsdp
        for s in range(seq):
            row = s // across * rows
            for z in range(fsdp):
                col = z * (FF // fsdp) + s % across * cols
                piece = acc2[row : row + rows, col : col + cols]
                gw_ref[s % 2, s // 2, 1, z] = piece.astype(BF16)


def write_pieces(sizes, ref, k, acc):
    seq, fsdp = sizes
    rows, cols = C // fsdp, FF // seq
    for s in range(seq):
        for z in range(fsdp):
            piece = acc[z * rows : z * rows + rows, s * cols : s * cols + cols]
            ref[s % 2, s // 2, k, z] = piece.astype(BF16)


def attn_bwd_kernel(sizes, dm_ref, x_ref, att_ref, proj_ref, p_ref, g_ref, s_ref, own_ref,
                    other_ref, perm_ref, permt_ref,
                    dx_ref, gw_ref, gqkvb_ref, gpb_ref, gg_ref, gs_ref, gbias_ref,
                    acc, dattw, attw, dqw, dkt, dvt, w_ref, sems):
    @pl.when(first_step())
    def _():
        fetch_weights(sizes, [by_columns(sizes, w_ref)], own_ref, other_ref, sems)
        acc[...] = jnp.zeros_like(acc)
        gqkvb_ref[...] = jnp.zeros_like(gqkvb_ref)
        gbias_ref[...] = jnp.zeros_like(gbias_ref)

    dm = dm_ref[...]
    dy = dm.astype(BF16)
    att = att_ref[...]
    accumulate(gpb_ref, col_sum(dy.astype(F32)))
    acc[:, 3 * C :] += dot_tn(att, dy)
    datt = dot_t(dy, w_ref[:, 3 * C :]).astype(BF16)
    dattw[...] = dot(perm_ref[...], datt).astype(BF16)
    attw[...] = dot(perm_ref[...], att).astype(BF16)

    masks = head_masks()
    ones = jnp.concatenate(masks, axis=0)
    low_half = lax.broadcasted_iota(jnp.int32, (HEAD, 128), 1) < PAD

    def one_window(w):
        rows = pl.ds(pl.multiple_of(w * PAD, PAD), PAD)
        dks, dvs = [], []
        for g in range(GROUPS):
            lanes = slice(128 * g, 128 * g + 128)
            wide = slice(256 * g, 256 * g + 256)
            q = proj_ref[rows, lanes]
            k = proj_ref[rows, C + 128 * g : C + 128 * g + 128]
            v = proj_ref[rows, 2 * C + 128 * g : 2 * C + 128 * g + 128]
            p = p_ref[rows, wide]
            da = dattw[rows, lanes]
            inner = (-(da.astype(F32) * attw[rows, lanes].astype(F32))).astype(BF16)
            left = jnp.concatenate([da, inner], axis=1)
            right = jnp.concatenate([spread(v, masks), ones], axis=1)
            ds = (p.astype(F32) * dot_t(left, right)).astype(BF16)
            gbias_ref[:, wide] += ds.astype(F32)
            dqw[rows, lanes] = (dot(ds, spread(k, masks)) * SCALE).astype(BF16)
            dks.append(dot_tn(q, ds))
            dvs.append(dot_tn(da, p))
        return dks, dvs

    def diagonal(first, second):
        parts = []
        for h in range(4):
            lanes = slice(128 * (h // 2), 128 * (h // 2) + 128)
            one = first[HEAD * h : HEAD * h + HEAD, lanes]
            two = second[HEAD * h : HEAD * h + HEAD, lanes]
            if h % 2 == 0:
                two = pltpu.roll(two, PAD, 1)
            else:
                one = pltpu.roll(one, PAD, 1)
            parts.append(jnp.where(low_half, one, two))
        return jnp.concatenate(parts, axis=0)

    def pair(i, carry):
        dk0, dv0 = one_window(2 * i)
        dk1, dv1 = one_window(2 * i + 1)
        cols = pl.ds(pl.multiple_of(i * 128, 128), 128)
        for g in range(GROUPS):
            dkt[128 * g : 128 * g + 128, cols] = (diagonal(dk0[g], dk1[g]) * SCALE).astype(BF16)
            dvt[128 * g : 128 * g + 128, cols] = diagonal(dv0[g], dv1[g]).astype(BF16)
        return carry

    lax.fori_loop(0, WPB // 2, pair, 0)
    permt = permt_ref[...]
    x = x_ref[...].astype(F32)
    xhat, inv = normalize(x)
    a = (xhat * g_ref[...] + s_ref[...]).astype(BF16)
    e = jnp.zeros((BAND, C), F32)

    for c in range(3):
        cols = slice(c * C, (c + 1) * C)
        if c == 0:
            dp = dot(permt, dqw[...])
        else:
            dp = dot_t(permt, (dkt if c == 1 else dvt)[...])
        gqkvb_ref[:, cols] += col_sum(dp)
        dp = dp.astype(BF16)
        acc[:, cols] += dot_tn(a, dp)
        e = e + dot_t(dp, w_ref[:, cols])
    accumulate(gg_ref, col_sum(e * xhat))
    accumulate(gs_ref, col_sum(e))
    dx_ref[...] = dm + norm_back(e, xhat, inv, g_ref[...])

    @pl.when(last_step())
    def _():
        write_pieces(sizes, gw_ref, 0, acc)


def band_spec(*shape):
    return pl.BlockSpec((None,) + shape, lambda i: (i,) + (0,) * len(shape))


def whole_spec(*shape):
    return pl.BlockSpec(shape, lambda i: (0,) * len(shape))


def params():
    return pltpu.CompilerParams(vmem_limit_bytes=60 << 20)


def cost(flops, bytes_accessed, transcendentals=0):
    return pl.CostEstimate(
        flops=int(flops), bytes_accessed=int(bytes_accessed), transcendentals=int(transcendentals)
    )


def shape(*dims, dtype=F32):
    return jax.ShapeDtypeStruct(dims, dtype)


def hbm_spec():
    return pl.BlockSpec(memory_space=pl.ANY)


def weight_scratch(sizes, *shapes):
    copies = sizes[0] * sizes[1] * len(shapes)
    return [pltpu.VMEM(s, BF16) for s in shapes] + [pltpu.SemaphoreType.DMA((copies,))]


def piece_shape(sizes, kinds):
    seq, fsdp = sizes
    return (2, seq // 2, kinds, fsdp, C // fsdp, FF // seq)


def attn_fwd(sizes, x, gain, shift, weights, qkvb, perm, permt, bias, mask, pb):
    n = x.shape[0]
    rolled = mask is not None
    in_specs = [
        band_spec(BAND, C), whole_spec(1, C), whole_spec(1, C), hbm_spec(), hbm_spec(),
        whole_spec(1, 3 * C), whole_spec(WROWS, BAND), whole_spec(BAND, WROWS),
        whole_spec(PAD, SCORES),
    ]
    args = [x, gain, shift, *weights, qkvb, perm, permt, bias]
    if rolled:
        kinds = mask.shape[0]
        in_specs.append(pl.BlockSpec((None, WPB, PAD, 256), lambda i: (i % kinds, 0, 0, 0)))
        args.append(mask)
    in_specs += [whole_spec(1, C)]
    args += [pb]
    return pl.pallas_call(
        functools.partial(attn_fwd_kernel, sizes, rolled),
        grid=(n,),
        in_specs=in_specs,
        out_specs=[band_spec(WROWS, 3 * C), band_spec(WROWS, SCORES), band_spec(BAND, C),
                   band_spec(BAND, C)],
        out_shape=[shape(n, WROWS, 3 * C, dtype=BF16), shape(n, WROWS, SCORES, dtype=BF16),
                   shape(n, BAND, C, dtype=BF16), shape(n, BAND, C)],
        scratch_shapes=[pltpu.VMEM((WROWS, C), BF16), *weight_scratch(sizes, (C, FF))],
        compiler_params=params(),
        cost_estimate=cost(n * 6e9, n * 5e6, n * 5e5),
        name="attn_fwd",
    )(*args)


def mlp_fwd(sizes, m, gain, shift, weights, b1, b2):
    n = m.shape[0]
    return pl.pallas_call(
        functools.partial(mlp_fwd_kernel, sizes),
        grid=(n,),
        in_specs=[band_spec(BAND, C), whole_spec(1, C), whole_spec(1, C), hbm_spec(), hbm_spec(),
                  whole_spec(1, FF), whole_spec(1, C)],
        out_specs=[band_spec(BAND, FF), band_spec(BAND, FF), band_spec(BAND, C)],
        out_shape=[shape(n, BAND, FF, dtype=BF16), shape(n, BAND, FF, dtype=BF16),
                   shape(n, BAND, C)],
        scratch_shapes=weight_scratch(sizes, (C, FF), (FF, C)),
        compiler_params=params(),
        cost_estimate=cost(n * 6e9, n * 5e6, n * 16e5),
        name="mlp_fwd",
    )(m, gain, shift, *weights, b1, b2)


def mlp_bwd(sizes, dh, m, act, slope, gain, shift, weights):
    n = m.shape[0]
    pieces = piece_shape(sizes, 2)
    return pl.pallas_call(
        functools.partial(mlp_bwd_kernel, sizes),
        grid=(n,),
        in_specs=[band_spec(BAND, C), band_spec(BAND, C), band_spec(BAND, FF), band_spec(BAND, FF),
                  whole_spec(1, C), whole_spec(1, C), hbm_spec(), hbm_spec()],
        out_specs=[band_spec(BAND, C), whole_spec(*pieces), whole_spec(1, FF),
                   whole_spec(1, C), whole_spec(1, C), whole_spec(1, C)],
        out_shape=[shape(n, BAND, C), shape(*pieces, dtype=BF16),
                   shape(1, FF), shape(1, C), shape(1, C), shape(1, C)],
        scratch_shapes=[pltpu.VMEM((C, FF), F32), pltpu.VMEM((C, FF), F32),
                        *weight_scratch(sizes, (C, FF), (FF, C))],
        compiler_params=params(),
        cost_estimate=cost(n * 12e9, n * 6e6),
        name="mlp_bwd",
    )(dh, m, act, slope, gain, shift, *weights)


def attn_bwd(sizes, dm, x, att, proj, p, gain, shift, weights, perm, permt):
    n = dm.shape[0]
    pieces = piece_shape(sizes, 1)
    return pl.pallas_call(
        functools.partial(attn_bwd_kernel, sizes),
        grid=(n,),
        in_specs=[band_spec(BAND, C), band_spec(BAND, C), band_spec(BAND, C),
                  band_spec(WROWS, 3 * C), band_spec(WROWS, SCORES), whole_spec(1, C),
                  whole_spec(1, C), hbm_spec(), hbm_spec(),
                  whole_spec(WROWS, BAND), whole_spec(BAND, WROWS)],
        out_specs=[band_spec(BAND, C), whole_spec(*pieces),
                   whole_spec(1, 3 * C), whole_spec(1, C), whole_spec(1, C), whole_spec(1, C),
                   whole_spec(PAD, SCORES)],
        out_shape=[shape(n, BAND, C), shape(*pieces, dtype=BF16),
                   shape(1, 3 * C), shape(1, C), shape(1, C), shape(1, C), shape(PAD, SCORES)],
        scratch_shapes=[pltpu.VMEM((C, FF), F32),
                        pltpu.VMEM((WROWS, C), BF16), pltpu.VMEM((WROWS, C), BF16),
                        pltpu.VMEM((WROWS, C), BF16), pltpu.VMEM((C, WROWS), BF16),
                        pltpu.VMEM((C, WROWS), BF16), *weight_scratch(sizes, (C, FF))],
        compiler_params=params(),
        cost_estimate=cost(n * 10e9, n * 6e6),
        name="attn_bwd",
    )(dm, x, att, proj, p, gain, shift, *weights, perm, permt)


def window_permutation(rolled):
    row = jnp.arange(WROWS, dtype=jnp.int32)
    window, cell = row // PAD, row % PAD
    col = window * WIN + cell % WIN
    if rolled:
        col = (col + SHIFT) % SIDE
    source = jnp.where(cell < WIN2, cell // WIN * SIDE + col, -1)
    token = jnp.arange(BAND, dtype=jnp.int32)
    perm = (source[:, None] == token[None, :]).astype(BF16)
    permt = (source[None, :] == token[:, None]).astype(BF16)
    return perm, permt


def padded_selector(rel_index):
    index = jnp.full((PAD, PAD), -1, jnp.int32).at[:WIN2, :WIN2].set(rel_index)
    return (index[:, :, None] == jnp.arange(BIAS_ROWS, dtype=jnp.int32)).astype(F32)


def score_bias(selector, table):
    bias = jnp.einsum("ijr,rh->ihj", selector, table, precision=highest) * LOG2E
    real = (jnp.arange(PAD) < WIN2)[None, None, :]
    return jnp.where(real, bias, NEG).reshape(PAD, SCORES)


def table_grad(selector, grad_bias):
    return jnp.einsum(
        "ijr,ihj->rh", selector, grad_bias.reshape(PAD, HEADS, PAD), precision=highest
    )


def score_mask(region_rows):
    rows = region_rows.shape[0]
    ids = region_rows.reshape(rows // WIN, WIN, WPB, WIN).transpose(0, 2, 1, 3)
    ids = ids.reshape(rows // WIN, WPB, WIN2)
    ids = jnp.pad(ids, ((0, 0), (0, 0), (0, PAD - WIN2)), constant_values=-1)
    real = jnp.arange(PAD) < WIN2
    blocked = (ids[..., :, None] != ids[..., None, :]) & real[:, None]
    mask = jnp.where(blocked, NEG, 0.0).astype(F32)
    return jnp.concatenate([mask] * 4, axis=-1)


def partner(block, bit):
    count = lax.axis_size("seq")
    return lax.ppermute(block, "seq", [(i, i ^ (1 << bit)) for i in range(count)])


def from_behind(block, distance):
    count = lax.axis_size("seq")
    return lax.ppermute(block, "seq", [((i - distance) % count, i) for i in range(count)])


def group_exchange(pieces):
    count = pieces.shape[0]
    position = lax.axis_index("seq")
    for bit in range(count.bit_length() - 1):
        flag = position // (1 << bit) % 2 == 1
        shaped = pieces.reshape((count // (2 << bit), 2, 1 << bit) + pieces.shape[1:])
        lower, upper = shaped[:, 0], shaped[:, 1]
        kept = jnp.where(flag, upper, lower)
        incoming = partner(jnp.where(flag, lower, upper).astype(BF16), bit).astype(pieces.dtype)
        first = jnp.where(flag, incoming, kept)
        second = jnp.where(flag, kept, incoming)
        pieces = jnp.stack([first, second], axis=1).reshape(pieces.shape)
    return pieces


def swap(block, axis, mask):
    count = lax.axis_size(axis)
    return lax.ppermute(block, axis, [(i, i ^ mask) for i in range(count)])


def gather_pieces(piece):
    seq, fsdp = lax.axis_size("seq"), lax.axis_size("fsdp")
    line = jnp.stack([piece] + [swap(piece, "fsdp", e) for e in range(1, fsdp)])
    own = jnp.stack([line] + [swap(line, "seq", 2 * d) for d in range(1, seq // 2)])
    return own, swap(own, "seq", 1)


def pick(values, index, axis=0):
    return lax.dynamic_index_in_dim(values, index, axis, keepdims=False)


def add_all(first, others):
    total = first.astype(F32)
    for other in others:
        total = total + other.astype(F32)
    return total.astype(first.dtype)


def in_order(values, me):
    for bit in range(values.shape[0].bit_length() - 1):
        shaped = values.reshape((-1, 2, 1 << bit) + values.shape[1:])
        flip = (me >> bit) & 1 == 1
        values = jnp.where(flip, shaped[:, ::-1], shaped).reshape(values.shape)
    return values


def scatter_pieces(pieces):
    seq, fsdp = lax.axis_size("seq"), lax.axis_size("fsdp")
    me, line = lax.axis_index("seq"), lax.axis_index("fsdp")
    plane, core = me // 2, me % 2
    part = add_all(pick(pieces, core), [swap(pick(pieces, 1 - core), "seq", 1)])
    part = add_all(pick(part, plane), [
        swap(pick(part, plane ^ d), "seq", 2 * d) for d in range(1, seq // 2)
    ])
    part = add_all(pick(part, line, 1), [
        swap(pick(part, line ^ e, 1), "fsdp", e) for e in range(1, fsdp)
    ])
    own = jnp.stack([part] + [swap(part, "seq", 2 * d) for d in range(1, seq // 2)])
    both = jnp.stack([own, swap(own, "seq", 1)])
    both = in_order(both, core)
    both = in_order(both.swapaxes(0, 1), plane)
    return both.reshape((seq,) + part.shape).astype(F32)


def sum_small(value):
    seq, fsdp = lax.axis_size("seq"), lax.axis_size("fsdp")
    for axis, count in (("seq", seq), ("fsdp", fsdp)):
        for bit in range(count.bit_length() - 1):
            value = value + swap(value, axis, 1 << bit)
    return value


def sum_small_all(values):
    sizes = [v.size for v in values]
    flat = jnp.concatenate([v.reshape(-1) for v in values])
    pad = -flat.size % 1024
    flat = sum_small(jnp.pad(flat, (0, pad)).reshape(-1, 128)).reshape(-1)
    out, start = [], 0
    for v, size in zip(values, sizes):
        out.append(flat[start : start + size].reshape(v.shape))
        start += size
    return out


def split_heads(w):
    return w.reshape(w.shape[0], HEADS, 3, HEAD).transpose(0, 2, 1, 3).reshape(w.shape)


def join_heads(w):
    return w.reshape(w.shape[0], 3, HEADS, HEAD).transpose(0, 2, 1, 3).reshape(w.shape)


def on_device(inputs, cotangent, region_ids, rel_index, ln1_gain, ln1_bias, qkv_w, q_bias, v_bias,
              rel_table, proj_w, proj_b, ln2_gain, ln2_bias, fc1_w, fc1_b, fc2_w, fc2_b):
    images, tokens, features = inputs.shape
    position = lax.axis_index("seq")
    group = 1
    while group * tokens % BAND:
        group *= 2
    per_group = images // group
    local = group * tokens
    bands = local // BAND

    def regroup(x):
        if group == 1:
            return x
        x = group_exchange(x.reshape(group, per_group, tokens, features))
        return x.transpose(1, 0, 2, 3).reshape(per_group, local, features)

    def ungroup(x):
        if group == 1:
            return x
        x = x.reshape(per_group, group, tokens, features).transpose(1, 0, 2, 3)
        return group_exchange(x).reshape(images, tokens, features)

    def roll_in(x):
        tail = from_behind(x[:, :HALO].astype(BF16), -group).astype(x.dtype)
        return jnp.concatenate([x[:, HALO:], tail], axis=1)

    def roll_out(x):
        head = from_behind(x[:, -HALO:].astype(BF16), group).astype(x.dtype)
        return jnp.concatenate([head, x[:, :-HALO]], axis=1)

    def as_bands(x):
        return x.reshape(per_group * bands, BAND, features)

    def as_images(x):
        return x.reshape(per_group, local, features)

    seq, fsdp = lax.axis_size("seq"), lax.axis_size("fsdp")
    sizes = (seq, fsdp)
    rows, cols, across = C // fsdp, FF // seq, seq // 4

    def piece(w, row, col):
        return lax.dynamic_slice(w, (row * rows, col * cols), (rows, cols))

    attn_w, mlp_w = [], []
    for l in range(LAYERS):
        joined = jnp.concatenate([split_heads(qkv_w[l]), proj_w[l]], axis=1)
        attn_w.append(gather_pieces(piece(joined, 0, position)[None]))
        mlp_w.append(gather_pieces(jnp.stack([
            piece(fc1_w[l], 0, position), piece(fc2_w[l], position // across, position % across),
        ])))

    selector = padded_selector(rel_index)
    region_rows = lax.dynamic_slice_in_dim(
        region_ids, position // group * bands * WIN, bands * WIN, 0
    )
    masks = (None, score_mask(region_rows))
    perms = (window_permutation(False), window_permutation(True))

    stream = regroup(inputs)
    upstream = roll_in(regroup(cotangent))
    saved = []
    for l in range(LAYERS):
        kind = l % 2
        if l > 0:
            stream = roll_in(stream) if kind else roll_out(stream)
        x = as_bands(stream)
        qkvb = jnp.concatenate([q_bias[l], jnp.zeros_like(q_bias[l]), v_bias[l]])[None]
        bias = score_bias(selector, rel_table[l])
        proj, p, att, m = attn_fwd(
            sizes, x, ln1_gain[l][None], ln1_bias[l][None], attn_w[l], qkvb, *perms[kind], bias,
            masks[kind], proj_b[l][None],
        )
        act, slope, h = mlp_fwd(
            sizes, m, ln2_gain[l][None], ln2_bias[l][None], mlp_w[l], fc1_b[l][None],
            fc2_b[l][None],
        )
        saved.append((x, proj, p, att, m, act, slope))
        stream = as_images(h)
    out = ungroup(roll_out(stream))

    big, small = [], []
    for l in reversed(range(LAYERS)):
        kind = l % 2
        x, proj, p, att, m, act, slope = saved[l]
        dm, gmlp, gb1, gb2, gg2, gs2 = mlp_bwd(
            sizes, as_bands(upstream), m, act, slope, ln2_gain[l][None], ln2_bias[l][None],
            mlp_w[l],
        )
        dx, gattn, gqkvb, gpb, gg1, gs1, gbias = attn_bwd(
            sizes, dm, x, att, proj, p, ln1_gain[l][None], ln1_bias[l][None], attn_w[l],
            *perms[kind],
        )
        upstream = as_images(dx)
        if l > 0:
            upstream = roll_out(upstream) if kind else roll_in(upstream)
        gattn, gmlp = scatter_pieces(gattn), scatter_pieces(gmlp)
        gattn = gattn[:, 0].transpose(1, 0, 2).reshape(rows, FF)
        gw1 = gmlp[:, 0].transpose(1, 0, 2).reshape(rows, FF)
        gw2 = gmlp[:, 1].reshape(fsdp, seq // fsdp, rows, cols).transpose(1, 3, 0, 2)
        big.insert(0, (
            join_heads(gattn[:, : 3 * C]), gattn[:, 3 * C :], gw1, gw2.reshape(FF // fsdp, C),
        ))
        small.insert(0, sum_small_all((
            gg1[0], gs1[0], gqkvb[0, :C], gqkvb[0, 2 * C :], table_grad(selector, gbias),
            gpb[0], gg2[0], gs2[0], gb1[0], gb2[0],
        )))
    grad_in = ungroup(upstream)
    small = [jnp.stack([layer[i] for layer in small]) for i in range(10)]
    big = [jnp.stack([layer[i] for layer in big]) for i in range(4)]
    return (
        out, grad_in, small[0], small[1], big[0], small[2], small[3], small[4], big[1], small[5],
        small[6], small[7], big[2], small[8], big[3], small[9],
    )


def solution(mesh):
    tokens = P("fsdp", "seq", None)
    matrix = P(None, "fsdp", None)
    in_specs = (
        tokens, tokens, P(), P(), P(), P(), matrix, P(), P(), P(), matrix, P(), P(), P(), matrix,
        P(), matrix, P(),
    )
    out_specs = (
        tokens, tokens, P(), P(), matrix, P(), P(), P(), matrix, P(), P(), P(), matrix, P(),
        matrix, P(),
    )
    return jax.shard_map(
        on_device, mesh=mesh, in_specs=in_specs, out_specs=out_specs, check_vma=False
    )
```
